128 devices in a mesh: wide: 16 (over y_lo, x, core), narrow: 8 (over z, y_hi).
Axes of the slice: x: 4, y: 4 (y_hi: 2, y_lo: 2; y = y_hi * 2 + y_lo), z: 4, core: 2. Of those that a mesh axis runs over, the one named last changes fastest.
Arguments:
- heads_output: bfloat16 [1024, 8192], P('narrow', 'wide'), may hold values from -6 to 6
- residual_in: bfloat16 [1024, 16384], P('wide', 'narrow'), may hold values from -6 to 6
- out_weight: bfloat16 [8192, 16384], P('wide', 'narrow'), may hold values from -0.0625 to 0.0625
- norm_gain: float32 [16384], P('narrow'), may hold values from 0.1 to 1.9
- gate_weight: bfloat16 [16384, 26624], P('narrow', 'wide'), may hold values from -0.046875 to 0.046875
- up_weight: bfloat16 [16384, 26624], P('narrow', 'wide'), may hold values from -0.046875 to 0.046875
Outputs:
- residual: float32 [1024, 16384], P('wide', 'narrow')
- hidden: float32 [1024, 26624], P('narrow', 'wide')
The draws below stay inside these ranges and needn't reach their ends.
All inputs are finite; a program needn't handle non-finite values.
Results may differ from the reference program's by a relative error of at most 0.0041.
Values may be sent and summed in bfloat16 or wider, within the bound.
A program may use at most 128 MiB of HBM per device.

```python
import jax
import jax.numpy as jnp
from jax import lax

D = 16384
FF = 26624
HEADS = 64
HEAD_DIM = 128
TOKENS = 1024


def spiked(values, rng, source, target, shards_of, factor):
    owner, partner = [(jnp.arange(values.shape[dim]) // (values.shape[dim] // shards_of)).reshape([-1 if axis == dim else 1 for axis in range(values.ndim)]) for dim in (source, target)]
    chosen = jax.random.permutation(rng, shards_of)[partner]
    strong = (owner == chosen) | (owner == (partner + shards_of // 2) % shards_of)
    return jnp.where(strong, factor * values, values)


def levels(rng, shape, cuts, smallest, largest):
    factor_of, own = 1.0, jax.random.fold_in(rng, 6)
    for axis_at, parts in cuts:
        steps = jnp.exp(jax.random.uniform(jax.random.fold_in(own, axis_at), (parts,), jnp.float32, smallest / len(cuts), largest / len(cuts)))
        factor_of = factor_of * jnp.repeat(steps, shape[axis_at] // parts).reshape([-1 if axis == axis_at else 1 for axis in range(len(shape))])
    return factor_of


def normal_values(key, dims, spread, most, cuts=(), dtype=jnp.bfloat16):
    loudness = levels(key, dims, cuts, -0.22, 0.18) if cuts else 1.0
    array = jax.random.normal(key, dims, jnp.float32) * spread * loudness
    return jnp.minimum(jnp.maximum(array, -most), most).astype(dtype)


def heavy_noise(own_key, extent, scale, reach, shards, heavy, held_as=jnp.bfloat16):
    values = scale * jax.random.normal(own_key, extent, jnp.float32)
    if shards:
        values = values * levels(own_key, extent, shards, -0.22, 0.18)
    return jnp.clip(spiked(values, jax.random.fold_in(own_key, 3), *heavy), -reach, reach).astype(held_as)


def setup_inputs(seed: int = 0) -> dict:
    splits = jax.random.split(jax.random.key(seed), 7)
    return {
        "heads_output": heavy_noise(splits[0], (TOKENS, HEADS * HEAD_DIM), 1.0, 6.0, ((0, 8), (1, 16)), (1, 0, 16, 2.0)),
        "residual_in": normal_values(splits[1], (TOKENS, D), 1.0, 6.0, ((0, 16), (1, 8))),
        "out_weight": normal_values(splits[2], (HEADS * HEAD_DIM, D), (HEADS * HEAD_DIM) ** -0.5, 0.0625, ((0, 16), (1, 8))),
        "norm_gain": jnp.clip(1.0 + 0.18 * jax.random.normal(splits[3], (D,), jnp.float32), 0.1, 1.9),
        "gate_weight": normal_values(splits[4], (D, FF), D ** -0.5, 0.046875, ((0, 8), (1, 16))),
        "up_weight": normal_values(splits[5], (D, FF), D ** -0.5, 0.046875, ((0, 8), (1, 16))),
    }


def reference(heads_output, residual_in, out_weight, norm_gain, gate_weight, up_weight):
    attended = jnp.dot(heads_output, out_weight, preferred_element_type=jnp.float32)
    residual = residual_in.astype(jnp.float32) + attended
    squares = lax.optimization_barrier(jnp.sum(residual * residual, axis=1))
    scale = 1.0 / jnp.sqrt(squares / D + 1e-05)
    normed = (residual * scale[:, None] * norm_gain).astype(jnp.bfloat16)
    gate = jnp.dot(normed, gate_weight, preferred_element_type=jnp.float32)
    up = jnp.dot(normed, up_weight, preferred_element_type=jnp.float32)
    hidden = jax.nn.silu(gate) * up
    return (residual, hidden)
```

```python
import functools

import jax
import jax.numpy as jnp
from jax import lax
from jax.experimental import pallas as pl
from jax.experimental.pallas import tpu as pltpu
from jax.sharding import PartitionSpec as P

D = 16384
MESH = pl.DeviceIdType.MESH
F32, BF16 = jnp.float32, jnp.bfloat16
CHUNKS = 4
TILE = 256


def body(C, heads_h, rin_h, wo_h, gain_ref, wg_h, wu_h, res_h, hid_h,
         heads, wo, wgu, rin, s2, acc, r2, rx1, rx2, rxd, ry, res, sq, xn,
         sb2, sb1, sbm, own, rz1, rz2, rzd, sy, ryz, hid,
         ld, st, h_s, h_r, c_s, c_r, x_s, x_r, y_s, y_r, q_s, q_r, g_s, g_r, k_s, k_r,
         z_s, z_r, v_s, v_r):
    R = 64 // C
    ff = wgu.shape[1]
    half = ff // 2
    wide = lax.axis_index("wide")
    narrow = lax.axis_index("narrow")
    ylo, x, core = wide // 8, (wide // 2) % 4, wide % 2
    z, yhi = narrow // 2, narrow % 2
    up1, dn1, op2 = (z + 1) % 4, (z + 3) % 4, (z + 2) % 4

    def at(ylo=ylo, x=x, core=core, z=z, yhi=yhi):
        return (ylo * 8 + x * 2 + core, z * 2 + yhi)

    nar = []
    for dz in range(4):
        for dy in range(2):
            if dz or dy:
                nar.append((at(z=(z + dz) % 4, yhi=(yhi + dy) % 2), ((z + 4 - dz) % 4) * 2 + (yhi + dy) % 2))
    wid = []
    for dx in range(4):
        for dy in range(2):
            if dx or dy:
                wid.append((at(x=(x + dx) % 4, ylo=(ylo + dy) % 2), ((ylo + dy) % 2) * 4 + (x + 4 - dx) % 4))
    sib = at(core=1 - core)

    def rcopy(src, dst, ssem, rsem, dev):
        return pltpu.make_async_remote_copy(src_ref=src, dst_ref=dst, send_sem=ssem, recv_sem=rsem,
                                            device_id=dev, device_id_type=MESH)

    sends = []

    def go(cp):
        cp.start()
        sends.append(cp)

    lh = pltpu.make_async_copy(heads_h, heads.at[narrow], ld.at[0])
    lo = pltpu.make_async_copy(wo_h, wo, ld.at[1])
    lr = pltpu.make_async_copy(rin_h, rin, ld.at[2])
    lg = pltpu.make_async_copy(wg_h, wgu.at[:, pl.ds(0, half)], ld.at[3])
    lu = pltpu.make_async_copy(wu_h, wgu.at[:, pl.ds(half, half)], ld.at[4])
    for cp in (lh, lo, lr, lg, lu):
        cp.start()

    bar = pltpu.get_barrier_semaphore()
    peers = [t for t, _ in nar] + [t for t, _ in wid] + [sib]
    for t in peers:
        pl.semaphore_signal(bar, inc=1, device_id=t, device_id_type=MESH)
    pl.semaphore_wait(bar, len(peers))

    lh.wait()
    rows = [pl.ds(c * R, R) for c in range(C)]
    mine = ylo * 4 + x

    def s_heads(c):
        for i, (t, _) in enumerate(nar):
            blk = heads.at[narrow, :, rows[c], :]
            go(rcopy(blk, blk, h_s.at[c, i], h_r.at[c, i], t))

    def s_proj(c):
        for i, (t, src) in enumerate(nar):
            blk = heads.at[src, :, rows[c], :]
            rcopy(blk, blk, h_s.at[c, i], h_r.at[c, i], t).wait_recv()
        if c == 0:
            lo.wait()
        for par, dst in ((1 - core, s2), (core, acc)):
            @pl.loop(0, 2048 // TILE)
            def _(j):
                cols = pl.ds(pl.multiple_of(j * TILE, TILE), TILE)
                a = heads[:, par, rows[c], :].reshape(8 * R, 512)
                p = jnp.dot(a, wo[:, cols], preferred_element_type=F32)
                dst[:, rows[c], cols] = p.reshape(8, R, TILE)
            if dst is s2:
                go(rcopy(s2.at[:, rows[c], :], r2.at[:, rows[c], :], c_s.at[c], c_r.at[c], sib))

    def xsteps(c):
        xp, xm = at(x=(x + 1) % 4), at(x=(x + 3) % 4)
        far, nx, pv = (x + 2) % 4, (x + 1) % 4, (x + 3) % 4
        r = rows[c]
        first = [rcopy(acc.at[far, r, :], rx1.at[0, r, :], x_s.at[c, 0], x_r.at[c, 0], xp),
                 rcopy(acc.at[4 + far, r, :], rx1.at[1, r, :], x_s.at[c, 1], x_r.at[c, 1], xm)]
        direct = [rcopy(acc.at[4 + nx, r, :], rxd.at[1, r, :], x_s.at[c, 2], x_r.at[c, 2], xp),
                  rcopy(acc.at[pv, r, :], rxd.at[0, r, :], x_s.at[c, 3], x_r.at[c, 3], xm)]
        second = [rcopy(rx1.at[0, r, :], rx2.at[0, r, :], x_s.at[c, 4], x_r.at[c, 4], xp),
                  rcopy(rx1.at[1, r, :], rx2.at[1, r, :], x_s.at[c, 5], x_r.at[c, 5], xm)]
        return first, direct, second, (nx, 4 + pv)

    def s_pair(c):
        rcopy(s2.at[:, rows[c], :], r2.at[:, rows[c], :], c_s.at[c], c_r.at[c], sib).wait_recv()

        @pl.loop(0, 8)
        def _(b):
            acc[b, rows[c], :] = acc[b, rows[c], :] + r2[b, rows[c], :]
        first, direct, _, _ = xsteps(c)
        for cp in first + direct:
            go(cp)

    def s_x2(c):
        first, _, second, mid = xsteps(c)
        for h in range(2):
            first[h].wait_recv()
            rx1[h, rows[c], :] = rx1[h, rows[c], :] + acc[mid[h], rows[c], :]
            go(second[h])

    def ycopy(c):
        return rcopy(acc.at[(1 - ylo) * 4 + x, rows[c], :], ry.at[rows[c], :], y_s.at[c], y_r.at[c], at(ylo=1 - ylo))

    def s_x3(c):
        _, direct, second, _ = xsteps(c)
        for cp in direct + second:
            cp.wait_recv()
        r = rows[c]
        for h in (1 - ylo, ylo):
            b = h * 4 + x
            acc[b, r, :] = acc[b, r, :] + rx2[h, r, :] + rxd[h, r, :]
            if h is not ylo:
                go(ycopy(c))

    def s_res(c):
        ycopy(c).wait_recv()
        if c == 0:
            lr.wait()
        r = rows[c]
        total = rin[r, :].astype(F32) + (acc[mine, r, :] + ry[r, :])
        res[r, :] = total
        out = pltpu.make_async_copy(res.at[r, :], res_h.at[r, :], st.at[0, c])
        out.start()
        outs.append(out)
        sq[narrow, r, :] = jnp.broadcast_to(jnp.sum(total * total, axis=1, keepdims=True), (R, 128))
        for i, (t, _) in enumerate(nar):
            blk = sq.at[narrow, r, :]
            go(rcopy(blk, blk, q_s.at[c, i], q_r.at[c, i], t))

    def s_norm(c):
        r = rows[c]
        for i, (t, src) in enumerate(nar):
            blk = sq.at[src, r, :]
            rcopy(blk, blk, q_s.at[c, i], q_r.at[c, i], t).wait_recv()
        ssum = sq[0, r, :]
        for i in range(1, 8):
            ssum = ssum + sq[i, r, :]
        scale = (1.0 / jnp.sqrt(ssum / D + 1e-05))[:, :1]
        xn[mine, core, r, :] = (res[r, :] * scale * gain_ref[...]).astype(BF16)
        blk = xn.at[mine, core, r, :]
        for i, (t, _) in enumerate(wid):
            go(rcopy(blk, blk, g_s.at[c, i], g_r.at[c, i], t))

    def s_gath(c):
        r = rows[c]
        for i, (t, src) in enumerate(wid):
            blk = xn.at[src, core, r, :]
            rcopy(blk, blk, g_s.at[c, i], g_r.at[c, i], t).wait_recv()
        blk = xn.at[:, core, r, :]
        go(rcopy(blk, blk, k_s.at[c], k_r.at[c], sib))

    def zsteps(c):
        zp, zm = at(z=up1), at(z=dn1)
        r = rows[c]
        first = [rcopy(sb2.at[0, :, r, :], rz1.at[0, :, r, :], z_s.at[c, 0], z_r.at[c, 0], zp),
                 rcopy(sb2.at[1, :, r, :], rz1.at[1, :, r, :], z_s.at[c, 1], z_r.at[c, 1], zm)]
        direct = [rcopy(sb1.at[1, :, r, :], rzd.at[1, :, r, :], z_s.at[c, 2], z_r.at[c, 2], zp),
                  rcopy(sbm.at[0, :, r, :], rzd.at[0, :, r, :], z_s.at[c, 3], z_r.at[c, 3], zm)]
        second = [rcopy(rz1.at[0, :, r, :], rz2.at[0, :, r, :], z_s.at[c, 4], z_r.at[c, 4], zp),
                  rcopy(rz1.at[1, :, r, :], rz2.at[1, :, r, :], z_s.at[c, 5], z_r.at[c, 5], zm)]
        return first, direct, second

    def s_mlp(c):
        r = rows[c]
        blk = xn.at[:, 1 - core, r, :]
        rcopy(blk, blk, k_s.at[c], k_r.at[c], sib).wait_recv()
        if c == 0:
            lg.wait()
            lu.wait()

        @pl.loop(0, ff // TILE)
        def _(j):
            cols = pl.ds(pl.multiple_of(j * TILE, TILE), TILE)
            w = wgu[:, cols]
            a = jnp.concatenate(
                [xn[pl.ds(b * 2, 2), :, r, :].reshape(4 * R, 2048) for b in (op2, up1, dn1, z)], axis=0)
            p = jnp.dot(a, w, preferred_element_type=F32).reshape(4, 2, 2, R, TILE)
            sb2[:, :, r, cols] = p[0].astype(BF16)
            sb1[:, :, r, cols] = p[1].astype(BF16)
            sbm[:, :, r, cols] = p[2].astype(BF16)
            own[:, :, r, cols] = p[3]
        first, direct, _ = zsteps(c)
        for cp in first + direct:
            go(cp)

    def s_z2(c):
        first, _, second = zsteps(c)
        for h, part in ((0, sb1), (1, sbm)):
            first[h].wait_recv()
            for j in range(2):
                rz1[h, j, rows[c], :] = (rz1[h, j, rows[c], :].astype(F32)
                                         + part[h, j, rows[c], :].astype(F32)).astype(BF16)
            go(second[h])

    def vcopy(c):
        return rcopy(sy.at[:, rows[c], :], ryz.at[:, rows[c], :], v_s.at[c], v_r.at[c], at(yhi=1 - yhi))

    def s_z3(c):
        _, direct, second = zsteps(c)
        for cp in direct + second:
            cp.wait_recv()
        r = rows[c]
        for j in range(2):
            h = 1 - yhi
            sy[j, r, :] = (own[h, j, r, :] + rz2[h, j, r, :].astype(F32) + rzd[h, j, r, :].astype(F32)).astype(BF16)
        go(vcopy(c))

    def s_out(c):
        vcopy(c).wait_recv()
        r = rows[c]
        for j in range(2):
            def total(cols):
                return (own[yhi, j, r, cols] + rz2[yhi, j, r, cols].astype(F32)
                        + rzd[yhi, j, r, cols].astype(F32) + ryz[j, r, cols].astype(F32))
            g = total(pl.ds(0, half))
            u = total(pl.ds(half, half))
            hid[j, r, :] = g / (1.0 + jnp.exp(-g)) * u
        out = pltpu.make_async_copy(hid.at[:, r, :], hid_h.at[:, r, :], st.at[1, c])
        out.start()
        outs.append(out)

    outs = []
    stage = [s_heads, s_proj, s_pair, s_x2, s_x3, s_res, s_norm, s_gath, s_mlp, s_z2, s_z3, s_out]
    for s, c in SCHEDULE(C, len(stage)):
        stage[s](c)
    for cp in sends:
        cp.wait_send()
    for cp in outs:
        cp.wait()


def SCHEDULE(C, n):
    return [(s, c) for s in range(n) for c in range(C)]


def on_device(heads_output, residual_in, out_weight, norm_gain, gate_weight, up_weight):
    C = CHUNKS
    dm, ffd = gate_weight.shape
    rows = residual_in.shape[0]
    anys = pl.BlockSpec(memory_space=pl.ANY)
    vm = pl.BlockSpec(memory_space=pltpu.VMEM)
    dma = pltpu.SemaphoreType.DMA
    V = pltpu.VMEM
    zb = (2, 2, rows, 2 * ffd)
    res, hid = pl.pallas_call(
        functools.partial(body, C),
        out_shape=(jax.ShapeDtypeStruct((rows, dm), F32), jax.ShapeDtypeStruct((2, rows, ffd), F32)),
        in_specs=[anys, anys, anys, vm, anys, anys],
        out_specs=(anys, anys),
        scratch_shapes=[
            V((8, 2, rows, 512), BF16), V((512, dm), BF16), V((dm, 2 * ffd), BF16), V((rows, dm), BF16),
            V((8, rows, dm), F32), V((8, rows, dm), F32), V((8, rows, dm), F32),
            V((2, rows, dm), F32), V((2, rows, dm), F32), V((2, rows, dm), F32), V((rows, dm), F32),
            V((rows, dm), F32), V((8, rows, 128), F32), V((8, 2, rows, dm), BF16),
            V(zb, BF16), V(zb, BF16), V(zb, BF16), V(zb, F32), V(zb, BF16), V(zb, BF16), V(zb, BF16),
            V((2, rows, 2 * ffd), BF16), V((2, rows, 2 * ffd), BF16), V((2, rows, ffd), F32),
            dma((5,)), dma((2, C)), dma((C, 7)), dma((C, 7)), dma((C,)), dma((C,)), dma((C, 6)), dma((C, 6)),
            dma((C,)), dma((C,)), dma((C, 7)), dma((C, 7)), dma((C, 7)), dma((C, 7)), dma((C,)), dma((C,)),
            dma((C, 6)), dma((C, 6)), dma((C,)), dma((C,)),
        ],
        compiler_params=pltpu.CompilerParams(collective_id=0, has_side_effects=True, vmem_limit_bytes=62 << 20),
        name="layer",
    )(heads_output.reshape(2, rows, 512), residual_in, out_weight, norm_gain.reshape(1, dm), gate_weight, up_weight)
    return res, hid.reshape(2 * rows, ffd)


def solution(mesh):
    return jax.shard_map(
        on_device, mesh=mesh,
        in_specs=(P("narrow", "wide"), P("wide", "narrow"), P("wide", "narrow"), P("narrow"),
                  P("narrow", "wide"), P("narrow", "wide")),
        out_specs=(P("wide", "narrow"), P("narrow", "wide")), check_vma=False)
```

```python
import functools

import jax
import jax.numpy as jnp
from jax import lax
from jax.experimental import pallas as pl
from jax.experimental.pallas import tpu as pltpu
from jax.sharding import PartitionSpec as P

D = 16384
MESH = pl.DeviceIdType.MESH
F32, BF16 = jnp.float32, jnp.bfloat16
CHUNKS = 4
PT = 1024
SPLIT = 1


ORDER = [
    (0, 0), (0, 2), (1, 0), (0, 1), (2, 0), (1, 1), (0, 3), (3, 0), (2, 1), (1, 2), (4, 0), (3, 1), (1, 3), (5, 0),
    (2, 2), (6, 0), (4, 1), (7, 0), (3, 2), (5, 1), (8, 0), (2, 3), (4, 2), (6, 1), (9, 0), (10, 0), (7, 1),
    (3, 3), (5, 2), (11, 0), (8, 1), (4, 3), (12, 0), (9, 1), (13, 0), (6, 2), (10, 1), (7, 2), (5, 3), (8, 2),
    (11, 1), (9, 2), (14, 0), (12, 1), (15, 0), (13, 1), (6, 3), (10, 2), (11, 2), (7, 3), (12, 2), (14, 1),
    (8, 3), (9, 3), (13, 2), (15, 1), (10, 3), (14, 2), (16, 0), (11, 3), (17, 0), (15, 2), (12, 3), (13, 3),
    (16, 2), (16, 1), (14, 3), (15, 3), (17, 2), (17, 1), (16, 3), (17, 3),
]


def body(C, heads_h, rin_h, wo_h, gain_ref, wg_h, wu_h, res_h, hid_h,
         heads, wo, wgu, rin, s2, acc, r2, rx1, rx2, rxd, ry, res, sq, xn,
         sb2, sd1, sdm, sp1, spm, own, rz1, rz2, rzd, sy, ryz, hid,
         ld, st, h_s, h_r, c_s, c_r, x_s, x_r, y_s, y_r, q_s, q_r, g_s, g_r, k_s, k_r,
         z_s, z_r, v_s, v_r):
    R = 64 // C
    ff = wgu.shape[1]
    half = ff // 2
    wide = lax.axis_index("wide")
    narrow = lax.axis_index("narrow")
    ylo, x, core = wide // 8, (wide // 2) % 4, wide % 2
    z, yhi = narrow // 2, narrow % 2
    up1, dn1, op2 = (z + 1) % 4, (z + 3) % 4, (z + 2) % 4

    def at(ylo=ylo, x=x, core=core, z=z, yhi=yhi):
        return (ylo * 8 + x * 2 + core, z * 2 + yhi)

    nar = []
    for dz in range(4):
        for dy in range(2):
            if dz or dy:
                nar.append((at(z=(z + dz) % 4, yhi=(yhi + dy) % 2), ((z + 4 - dz) % 4) * 2 + (yhi + dy) % 2))
    sib = at(core=1 - core)

    sends, got = [], set()

    class rcopy:
        def __init__(self, src, dst, sems, idx, dev):
            self.key = (id(sems[0]),) + idx
            self.make = lambda: pltpu.make_async_remote_copy(
                src_ref=src, dst_ref=dst, send_sem=sems[0].at[idx], recv_sem=sems[1].at[idx],
                device_id=dev, device_id_type=MESH)

        def wait_recv(self):
            got.add(self.key)
            self.make().wait_recv()

    def go(cp):
        cp.make().start()
        sends.append(cp)

    lh = pltpu.make_async_copy(heads_h, heads.at[narrow], ld.at[0])
    lo = pltpu.make_async_copy(wo_h, wo, ld.at[1])
    lr = pltpu.make_async_copy(rin_h, rin, ld.at[2])
    cut = half // 256 * 128 + 128
    span = ((0, cut), (cut, half))
    gcols = [pl.ds(2 * a, 2 * (b - a)) for a, b in span]
    lw = []
    for g, (a, b) in enumerate(span):
        lw.append([pltpu.make_async_copy(w.at[:, pl.ds(a, b - a)], wgu.at[:, pl.ds(2 * a + o * (b - a), b - a)],
                                         ld.at[3 + 2 * g + o]) for o, w in enumerate((wg_h, wu_h))])
    for cp in [lh, lo, lr] + lw[0] + lw[1]:
        cp.start()

    bar = pltpu.get_barrier_semaphore()
    peers = [t for t, _ in nar] + [at(x=(x + 1) % 4), at(x=(x + 3) % 4), at(ylo=1 - ylo), sib]
    for t in peers:
        pl.semaphore_signal(bar, inc=1, device_id=t, device_id_type=MESH)
    pl.semaphore_wait(bar, len(peers))

    lh.wait()
    rows = [pl.ds(c * R, R) for c in range(C)]
    mine = ylo * 4 + x

    def s_heads(c):
        for i, (t, _) in enumerate(nar):
            blk = heads.at[narrow, :, rows[c], :]
            go(rcopy(blk, blk, (h_s, h_r), (c, i,), t))

    def s_proj(c):
        for i, (t, src) in enumerate(nar):
            blk = heads.at[src, :, rows[c], :]
            rcopy(blk, blk, (h_s, h_r), (c, i,), t).wait_recv()
        if c == 0:
            lo.wait()

        @pl.loop(0, 2048 // PT)
        def _(j):
            cols = pl.ds(pl.multiple_of(j * PT, PT), PT)
            a = jnp.concatenate([heads[:, p, rows[c], :].reshape(8 * R, 512) for p in (1 - core, core)], axis=0)
            p = jnp.dot(a, wo[:, cols], preferred_element_type=F32)
            s2[:, rows[c], cols] = p[:8 * R].reshape(8, R, PT)
            acc[:, rows[c], cols] = p[8 * R:].reshape(8, R, PT)
        go(rcopy(s2.at[:, rows[c], :], r2.at[:, rows[c], :], (c_s, c_r), (c,), sib))

    def xsteps(c):
        xp, xm = at(x=(x + 1) % 4), at(x=(x + 3) % 4)
        far, nx, pv = (x + 2) % 4, (x + 1) % 4, (x + 3) % 4
        r = rows[c]
        first = [rcopy(acc.at[far, r, :], rx1.at[0, r, :], (x_s, x_r), (c, 0,), xp),
                 rcopy(acc.at[4 + far, r, :], rx1.at[1, r, :], (x_s, x_r), (c, 1,), xm)]
        direct = [rcopy(acc.at[4 + nx, r, :], rxd.at[1, r, :], (x_s, x_r), (c, 2,), xp),
                  rcopy(acc.at[pv, r, :], rxd.at[0, r, :], (x_s, x_r), (c, 3,), xm)]
        second = [rcopy(rx1.at[0, r, :], rx2.at[0, r, :], (x_s, x_r), (c, 4,), xp),
                  rcopy(rx1.at[1, r, :], rx2.at[1, r, :], (x_s, x_r), (c, 5,), xm)]
        return first, direct, second, (nx, 4 + pv)

    def s_pair(c):
        rcopy(s2.at[:, rows[c], :], r2.at[:, rows[c], :], (c_s, c_r), (c,), sib).wait_recv()

        @pl.loop(0, 8)
        def _(b):
            acc[b, rows[c], :] = acc[b, rows[c], :] + r2[b, rows[c], :]
        first, direct, _, _ = xsteps(c)
        for cp in first + direct:
            go(cp)

    def s_x2(c):
        first, _, second, mid = xsteps(c)
        for h in range(2):
            first[h].wait_recv()
            rx1[h, rows[c], :] = rx1[h, rows[c], :] + acc[mid[h], rows[c], :]
            go(second[h])

    def ycopy(c):
        return rcopy(acc.at[(1 - ylo) * 4 + x, rows[c], :], ry.at[rows[c], :], (y_s, y_r), (c,), at(ylo=1 - ylo))

    def s_x3(c):
        _, direct, second, _ = xsteps(c)
        for cp in direct + second:
            cp.wait_recv()
        r = rows[c]
        for h in (1 - ylo, ylo):
            b = h * 4 + x
            acc[b, r, :] = acc[b, r, :] + rx2[h, r, :] + rxd[h, r, :]
            if h is not ylo:
                go(ycopy(c))

    def s_res(c):
        ycopy(c).wait_recv()
        if c == 0:
            lr.wait()
        r = rows[c]
        total = rin[r, :].astype(F32) + (acc[mine, r, :] + ry[r, :])
        res[r, :] = total
        out = pltpu.make_async_copy(res.at[r, :], res_h.at[r, :], st.at[0, c])
        out.start()
        outs.append(out)
        sq[narrow, r, :] = jnp.broadcast_to(jnp.sum(total * total, axis=1, keepdims=True), (R, 128))
        for i, (t, _) in enumerate(nar):
            blk = sq.at[narrow, r, :]
            go(rcopy(blk, blk, (q_s, q_r), (c, i,), t))

    def s_norm(c):
        r = rows[c]
        for i, (t, src) in enumerate(nar):
            blk = sq.at[src, r, :]
            rcopy(blk, blk, (q_s, q_r), (c, i,), t).wait_recv()
        ssum = sq[0, r, :]
        for i in range(1, 8):
            ssum = ssum + sq[i, r, :]
        scale = (1.0 / jnp.sqrt(ssum / D + 1e-05))[:, :1]
        xn[mine, core, r, :] = (res[r, :] * scale * gain_ref[...]).astype(BF16)
        for i, t in ((0, xp), (1, xm), (2, yp)):
            go(gcopy(c, mine, i, t))
        go(kcopy(c, 0, mine))

    xp, xm, yp = at(x=(x + 1) % 4), at(x=(x + 3) % 4), at(ylo=1 - ylo)
    yours = (1 - ylo) * 4 + x

    def gcopy(c, b, i, t):
        blk = xn.at[b, core, rows[c], :]
        return rcopy(blk, blk, (g_s, g_r), (c, i), t)

    def kcopy(c, i, b):
        blk = xn.at[b, core, rows[c], :]
        return rcopy(blk, blk, (k_s, k_r), (c, i), sib)

    pvx, nxx, far = (x + 3) % 4, (x + 1) % 4, (x + 2) % 4
    held = [mine, ylo * 4 + pvx, ylo * 4 + nxx, yours, (1 - ylo) * 4 + pvx, (1 - ylo) * 4 + nxx, far, 4 + far]

    def s_g2(c):
        gcopy(c, yours, 2, yp).wait_recv()
        go(gcopy(c, yours, 3, xp))
        go(gcopy(c, yours, 4, xm))
        go(kcopy(c, 3, yours))

    def s_g3(c):
        gcopy(c, held[1], 0, xp).wait_recv()
        gcopy(c, held[2], 1, xm).wait_recv()
        gcopy(c, held[4], 3, xp).wait_recv()
        gcopy(c, held[5], 4, xm).wait_recv()
        go(gcopy(c, pvx, 5, xp))
        go(gcopy(c, 4 + nxx, 6, xm))
        for k in (1, 2, 4, 5):
            go(kcopy(c, k, held[k]))

    def s_gath(c):
        gcopy(c, far, 5, xp).wait_recv()
        gcopy(c, 4 + far, 6, xm).wait_recv()
        for k in (6, 7):
            go(kcopy(c, k, held[k]))

    zp, zm = at(z=up1), at(z=dn1)

    def zsteps(c, g):
        r, w = rows[c], gcols[g]

        def cp(src, dst, i, t):
            return rcopy(src, dst, (z_s, z_r), (c, g, i), t)
        first = [cp(sb2.at[0, :, r, w], rz1.at[0, :, r, w], 0, zp), cp(sb2.at[1, :, r, w], rz1.at[1, :, r, w], 1, zm)]
        direct = [cp(sdm.at[:, r, w], rzd.at[0, :, r, w], 3, zm), cp(sd1.at[:, r, w], rzd.at[1, :, r, w], 2, zp)]
        second = [cp(rz1.at[0, :, r, w], rz2.at[0, :, r, w], 4, zp), cp(rz1.at[1, :, r, w], rz2.at[1, :, r, w], 5, zm)]
        return first, direct, second

    def mlp(c, g):
        r = rows[c]
        if g == 0:
            for k in range(8):
                blk = xn.at[held[k], 1 - core, r, :]
                rcopy(blk, blk, (k_s, k_r), (c, k), sib).wait_recv()
        if c == 0:
            for cp in lw[g]:
                cp.wait()
        base, tile = 2 * span[g][0], 2 * (span[g][1] - span[g][0]) // SPLIT

        @pl.loop(0, SPLIT)
        def _(j):
            cols = pl.ds(pl.multiple_of(base + j * tile, 128), tile)
            a = jnp.concatenate(
                [xn[pl.ds(b * 2, 2), :, r, :].reshape(4 * R, 2048) for b in (op2, up1, dn1, z)], axis=0)
            p = jnp.dot(a, wgu[:, cols], preferred_element_type=F32).reshape(4, 2, 2, R, tile)
            sb2[:, :, r, cols] = p[0].astype(BF16)
            sp1[:, r, cols] = p[1, 0]
            sd1[:, r, cols] = p[1, 1].astype(BF16)
            sdm[:, r, cols] = p[2, 0].astype(BF16)
            spm[:, r, cols] = p[2, 1]
            own[:, :, r, cols] = p[3]
        first, direct, _ = zsteps(c, g)
        for cp in first + direct:
            go(cp)

    def z2(c, g):
        first, _, second = zsteps(c, g)
        r, w = rows[c], gcols[g]
        for h, part in ((0, sp1), (1, spm)):
            first[h].wait_recv()
            for j in range(2):
                rz1[h, j, r, w] = (rz1[h, j, r, w].astype(F32) + part[j, r, w]).astype(BF16)
            go(second[h])

    def vcopy(c, g):
        return rcopy(sy.at[:, rows[c], gcols[g]], ryz.at[:, rows[c], gcols[g]], (v_s, v_r), (c, g), at(yhi=1 - yhi))

    def z3(c, g):
        _, direct, second = zsteps(c, g)
        for cp in direct + second:
            cp.wait_recv()
        r, w, h = rows[c], gcols[g], 1 - yhi
        for j in range(2):
            sy[j, r, w] = (own[h, j, r, w] + rz2[h, j, r, w].astype(F32) + rzd[h, j, r, w].astype(F32)).astype(BF16)
        go(vcopy(c, g))

    def out(c, g):
        vcopy(c, g).wait_recv()
        r, (a, b) = rows[c], span[g]
        for j in range(2):
            def total(o):
                w = pl.ds(2 * a + o * (b - a), b - a)
                return (own[yhi, j, r, w] + rz2[yhi, j, r, w].astype(F32)
                        + rzd[yhi, j, r, w].astype(F32) + ryz[j, r, w].astype(F32))
            v, u = total(0), total(1)
            hid[j, r, pl.ds(a, b - a)] = v / (1.0 + jnp.exp(-v)) * u
        cp = pltpu.make_async_copy(hid.at[:, r, pl.ds(a, b - a)], hid_h.at[:, r, pl.ds(a, b - a)], st.at[1 + g, c])
        cp.start()
        outs.append(cp)

    outs = []
    def grouped(f):
        return [functools.partial(f, g=0), functools.partial(f, g=1)]
    stage = [s_heads, s_proj, s_pair, s_x2, s_x3, s_res, s_norm, s_g2, s_g3, s_gath,
             *grouped(mlp), *grouped(z2), *grouped(z3), *grouped(out)]
    for s, c in ORDER:
        stage[s](c)
    for cp in sends:
        cp.make().wait_send()
    for cp in outs:
        cp.wait()


def on_device(heads_output, residual_in, out_weight, norm_gain, gate_weight, up_weight):
    C = CHUNKS
    dm, ffd = gate_weight.shape
    rows = residual_in.shape[0]
    anys = pl.BlockSpec(memory_space=pl.ANY)
    vm = pl.BlockSpec(memory_space=pltpu.VMEM)
    dma = pltpu.SemaphoreType.DMA
    V = pltpu.VMEM
    zb, zh = (2, 2, rows, 2 * ffd), (2, rows, 2 * ffd)
    res, hid = pl.pallas_call(
        functools.partial(body, C),
        out_shape=(jax.ShapeDtypeStruct((rows, dm), F32), jax.ShapeDtypeStruct((2, rows, ffd), F32)),
        in_specs=[anys, anys, anys, vm, anys, anys],
        out_specs=(anys, anys),
        scratch_shapes=[
            V((8, 2, rows, 512), BF16), V((512, dm), BF16), V((dm, 2 * ffd), BF16), V((rows, dm), BF16),
            V((8, rows, dm), F32), V((8, rows, dm), F32), V((8, rows, dm), F32),
            V((2, rows, dm), F32), V((2, rows, dm), F32), V((2, rows, dm), F32), V((rows, dm), F32),
            V((rows, dm), F32), V((8, rows, 128), F32), V((8, 2, rows, dm), BF16),
            V(zb, BF16), V(zh, BF16), V(zh, BF16), V(zh, F32), V(zh, F32), V(zb, F32), V(zb, BF16), V(zb, BF16), V(zb, BF16),
            V((2, rows, 2 * ffd), BF16), V((2, rows, 2 * ffd), BF16), V((2, rows, ffd), F32),
            dma((7,)), dma((3, C)), dma((C, 7)), dma((C, 7)), dma((C,)), dma((C,)), dma((C, 6)), dma((C, 6)),
            dma((C,)), dma((C,)), dma((C, 7)), dma((C, 7)), dma((C, 7)), dma((C, 7)), dma((C, 8)), dma((C, 8)),
            dma((C, 2, 6)), dma((C, 2, 6)), dma((C, 2)), dma((C, 2)),
        ],
        compiler_params=pltpu.CompilerParams(collective_id=0, has_side_effects=True, vmem_limit_bytes=62 << 20),
        name="layer",
    )(heads_output.reshape(2, rows, 512), residual_in, out_weight, norm_gain.reshape(1, dm), gate_weight, up_weight)
    return res, hid.reshape(2 * rows, ffd)


def solution(mesh):
    return jax.shard_map(
        on_device, mesh=mesh,
        in_specs=(P("narrow", "wide"), P("wide", "narrow"), P("wide", "narrow"), P("narrow"),
                  P("narrow", "wide"), P("narrow", "wide")),
        out_specs=(P("wide", "narrow"), P("narrow", "wide")), check_vma=False)
```

```python
import functools

import jax
import jax.numpy as jnp
from jax import lax
from jax.experimental import pallas as pl
from jax.experimental.pallas import tpu as pltpu
from jax.sharding import PartitionSpec as P

D = 16384
MESH = pl.DeviceIdType.MESH
F32, BF16 = jnp.float32, jnp.bfloat16
SIZES = (8, 8, 16, 16, 8, 8)
DIRECT = (True, False, False, False, False, False)
PT = 1024
SPLIT = 1
HAND = 2


ORDER = [
    (0, 0), (0, 1), (0, 2), (1, 0), (2, 0), (1, 1), (1, 2), (2, 1), (0, 5), (3, 0), (0, 3), (3, 1), (2, 2), (4, 0),
    (1, 3), (5, 0), (3, 2), (2, 3), (4, 1), (0, 4), (6, 0), (1, 5), (5, 1), (4, 2), (1, 4), (7, 0), (6, 1), (3, 3),
    (5, 2), (7, 1), (8, 0), (2, 4), (9, 0), (6, 2), (4, 3), (8, 1), (10, 0), (7, 2), (2, 5), (11, 0), (9, 1),
    (3, 4), (5, 3), (12, 0), (8, 2), (10, 1), (13, 0), (6, 3), (11, 1), (3, 5), (9, 2), (4, 4), (12, 1), (7, 3),
    (10, 2), (5, 4), (8, 3), (4, 5), (13, 1), (14, 0), (11, 2), (9, 3), (5, 5), (6, 4), (12, 2), (10, 3), (7, 4),
    (13, 2), (11, 3), (6, 5), (8, 4), (7, 5), (15, 0), (9, 4), (10, 4), (12, 3), (13, 3), (14, 2), (16, 0), (8, 5),
    (17, 0), (11, 4), (15, 2), (12, 4), (9, 5), (14, 1), (10, 5), (14, 3), (16, 2), (11, 5), (17, 2), (15, 1),
    (13, 4), (12, 5), (16, 1), (14, 4), (15, 3), (16, 3), (13, 5), (15, 4), (17, 1), (14, 5), (16, 4), (15, 5),
    (17, 4), (16, 5), (17, 3), (17, 5),
]


def body(C, heads_h, rin_h, wo_h, gain_ref, wg_h, wu_h, res_h, hid_h,
         heads, wo, wgu, rin, s2, acc, r2, rx1, rx2, rxd, ry, res, sq, xn,
         sb2, sd1, sdm, sp1, spm, own, rz1, rz2, rzd, sy, ryz, hid,
         ld, st, h_s, h_r, c_s, c_r, x_s, x_r, y_s, y_r, q_s, q_r, g_s, g_r, k_s, k_r,
         z_s, z_r, v_s, v_r):
    ff = wgu.shape[1]
    half = ff // 2
    wide = lax.axis_index("wide")
    narrow = lax.axis_index("narrow")
    ylo, x, core = wide // 8, (wide // 2) % 4, wide % 2
    z, yhi = narrow // 2, narrow % 2
    up1, dn1, op2 = (z + 1) % 4, (z + 3) % 4, (z + 2) % 4

    def at(ylo=ylo, x=x, core=core, z=z, yhi=yhi):
        return (ylo * 8 + x * 2 + core, z * 2 + yhi)

    nar = []
    for dz in range(4):
        for dy in range(2):
            if dz or dy:
                nar.append((at(z=(z + dz) % 4, yhi=(yhi + dy) % 2), ((z + 4 - dz) % 4) * 2 + (yhi + dy) % 2))
    sib = at(core=1 - core)

    sends, got = [], set()

    class rcopy:
        def __init__(self, src, dst, sems, idx, dev, ridx=None):
            self.key = (id(sems[0]),) + idx
            self.make = lambda: pltpu.make_async_remote_copy(
                src_ref=src, dst_ref=dst, send_sem=sems[0].at[idx], recv_sem=sems[1].at[idx if ridx is None else ridx],
                device_id=dev, device_id_type=MESH)

        def wait_recv(self):
            got.add(self.key)
            self.make().wait_recv()

    def go(cp):
        cp.make().start()
        sends.append(cp)

    lh = pltpu.make_async_copy(heads_h, heads.at[narrow], ld.at[0])
    lo = pltpu.make_async_copy(wo_h, wo, ld.at[1])
    lr = pltpu.make_async_copy(rin_h, rin, ld.at[2])
    cut = half // 256 * 128 + 128
    span = ((0, cut), (cut, half))
    gcols = [pl.ds(2 * a, 2 * (b - a)) for a, b in span]
    lw = []
    for g, (a, b) in enumerate(span):
        lw.append([pltpu.make_async_copy(w.at[:, pl.ds(a, b - a)], wgu.at[:, pl.ds(2 * a + o * (b - a), b - a)],
                                         ld.at[3 + 2 * g + o]) for o, w in enumerate((wg_h, wu_h))])
    for cp in [lh, lo]:
        cp.start()

    bar = pltpu.get_barrier_semaphore()
    peers = [t for t, _ in nar] + [at(x=(x + dx) % 4, ylo=yy) for dx in (1, 2, 3) for yy in (ylo, 1 - ylo)] + [at(ylo=1 - ylo), sib]
    for t in peers:
        pl.semaphore_signal(bar, inc=1, device_id=t, device_id_type=MESH)
    pl.semaphore_wait(bar, len(peers))

    lh.wait()
    rows = [pl.ds(sum(SIZES[:c]), SIZES[c]) for c in range(C)]
    mine = ylo * 4 + x

    def s_heads(c):
        for i, (t, _) in enumerate(nar):
            blk = heads.at[narrow, :, rows[c], :]
            go(rcopy(blk, blk, (h_s, h_r), (c, i,), t))

    def s_proj(c):
        for i, (t, src) in enumerate(nar):
            blk = heads.at[src, :, rows[c], :]
            rcopy(blk, blk, (h_s, h_r), (c, i,), t).wait_recv()
        if c == 0:
            lo.wait()
            for cp in [lr] + lw[0] + lw[1]:
                cp.start()

        @pl.loop(0, 2048 // PT)
        def _(j):
            cols = pl.ds(pl.multiple_of(j * PT, PT), PT)
            a = jnp.concatenate([heads[:, p, rows[c], :].reshape(8 * SIZES[c], 512) for p in (1 - core, core)], axis=0)
            p = jnp.dot(a, wo[:, cols], preferred_element_type=F32)
            s2[:, rows[c], cols] = p[:8 * SIZES[c]].reshape(8, SIZES[c], PT)
            acc[:, rows[c], cols] = p[8 * SIZES[c]:].reshape(8, SIZES[c], PT)
        go(rcopy(s2.at[:, rows[c], :], r2.at[:, rows[c], :], (c_s, c_r), (c,), sib))

    def xsteps(c):
        xp, xm = at(x=(x + 1) % 4), at(x=(x + 3) % 4)
        far, nx, pv = (x + 2) % 4, (x + 1) % 4, (x + 3) % 4
        r = rows[c]
        first = [rcopy(acc.at[far, r, :], rx1.at[0, r, :], (x_s, x_r), (c, 0,), xp),
                 rcopy(acc.at[4 + far, r, :], rx1.at[1, r, :], (x_s, x_r), (c, 1,), xm)]
        direct = [rcopy(acc.at[4 + nx, r, :], rxd.at[1, r, :], (x_s, x_r), (c, 2,), xp),
                  rcopy(acc.at[pv, r, :], rxd.at[0, r, :], (x_s, x_r), (c, 3,), xm)]
        second = [rcopy(rx1.at[0, r, :], rx2.at[0, r, :], (x_s, x_r), (c, 4,), xp),
                  rcopy(rx1.at[1, r, :], rx2.at[1, r, :], (x_s, x_r), (c, 5,), xm)]
        return first, direct, second, (nx, 4 + pv)

    def s_pair(c):
        rcopy(s2.at[:, rows[c], :], r2.at[:, rows[c], :], (c_s, c_r), (c,), sib).wait_recv()

        @pl.loop(0, 8)
        def _(b):
            acc[b, rows[c], :] = acc[b, rows[c], :] + r2[b, rows[c], :]
        first, direct, _, _ = xsteps(c)
        for cp in first + direct:
            go(cp)

    def s_x2(c):
        first, _, second, mid = xsteps(c)
        for h in range(2):
            first[h].wait_recv()
            rx1[h, rows[c], :] = rx1[h, rows[c], :] + acc[mid[h], rows[c], :]
            go(second[h])

    def ycopy(c):
        return rcopy(acc.at[(1 - ylo) * 4 + x, rows[c], :], ry.at[rows[c], :], (y_s, y_r), (c,), at(ylo=1 - ylo))

    def s_x3(c):
        _, direct, second, _ = xsteps(c)
        for cp in direct + second:
            cp.wait_recv()
        r = rows[c]
        for h in (1 - ylo, ylo):
            b = h * 4 + x
            acc[b, r, :] = acc[b, r, :] + rx2[h, r, :] + rxd[h, r, :]
            if h is not ylo:
                go(ycopy(c))

    def s_res(c):
        ycopy(c).wait_recv()
        if c == 0:
            lr.wait()
        r = rows[c]
        total = rin[r, :].astype(F32) + (acc[mine, r, :] + ry[r, :])
        res[r, :] = total
        out = pltpu.make_async_copy(res.at[r, :], res_h.at[r, :], st.at[0, c])
        out.start()
        outs.append(out)
        sq[narrow, r, :] = jnp.broadcast_to(jnp.sum(total * total, axis=1, keepdims=True), (SIZES[c], 128))
        for i, (t, _) in enumerate(nar):
            blk = sq.at[narrow, r, :]
            go(rcopy(blk, blk, (q_s, q_r), (c, i,), t))

    def s_norm(c):
        r = rows[c]
        for i, (t, src) in enumerate(nar):
            blk = sq.at[src, r, :]
            rcopy(blk, blk, (q_s, q_r), (c, i,), t).wait_recv()
        ssum = sq[0, r, :]
        for i in range(1, 8):
            ssum = ssum + sq[i, r, :]
        scale = (1.0 / jnp.sqrt(ssum / D + 1e-05))[:, :1]
        xn[mine, core, r, :] = (res[r, :] * scale * gain_ref[...]).astype(BF16)
        for i, t in ((0, xp), (1, xm), (2, yp)):
            go(gcopy(c, mine, i, t))
        if DIRECT[c]:
            other = 1 - ylo
            for i, ri, t in ((3, 3, at(x=nxx, ylo=other)), (4, 4, at(x=pvx, ylo=other)),
                             (5, 5 + ylo, at(x=far)), (6, 5 + ylo, at(x=far, ylo=other))):
                go(gcopy(c, mine, i, t, ri))
        go(kcopy(c, 0, mine))

    xp, xm, yp = at(x=(x + 1) % 4), at(x=(x + 3) % 4), at(ylo=1 - ylo)
    yours = (1 - ylo) * 4 + x

    def gcopy(c, b, i, t, ri=None):
        blk = xn.at[b, core, rows[c], :]
        return rcopy(blk, blk, (g_s, g_r), (c, i), t, None if ri is None else (c, ri))

    def kcopy(c, i, b):
        blk = xn.at[b, core, rows[c], :]
        return rcopy(blk, blk, (k_s, k_r), (c, i), sib)

    pvx, nxx, far = (x + 3) % 4, (x + 1) % 4, (x + 2) % 4
    held = [mine, ylo * 4 + pvx, ylo * 4 + nxx, yours, (1 - ylo) * 4 + pvx, (1 - ylo) * 4 + nxx, far, 4 + far]

    def s_g2(c):
        gcopy(c, yours, 2, yp).wait_recv()
        if not DIRECT[c]:
            go(gcopy(c, yours, 3, xp))
            go(gcopy(c, yours, 4, xm))
        go(kcopy(c, 3, yours))

    def s_g3(c):
        gcopy(c, held[1], 0, xp).wait_recv()
        gcopy(c, held[2], 1, xm).wait_recv()
        gcopy(c, held[4], 3, xp).wait_recv()
        gcopy(c, held[5], 4, xm).wait_recv()
        if not DIRECT[c]:
            go(gcopy(c, pvx, 5, xp))
            go(gcopy(c, 4 + nxx, 6, xm))
        for k in (1, 2, 4, 5):
            go(kcopy(c, k, held[k]))

    def s_gath(c):
        gcopy(c, far, 5, xp).wait_recv()
        gcopy(c, 4 + far, 6, xm).wait_recv()
        for k in (6, 7):
            go(kcopy(c, k, held[k]))

    zp, zm = at(z=up1), at(z=dn1)

    def zsteps(c, g):
        r, w = rows[c], gcols[g]

        def cp(src, dst, i, t):
            return rcopy(src, dst, (z_s, z_r), (c, g, i), t)
        first = [cp(sb2.at[0, :, r, w], rz1.at[0, :, r, w], 0, zp), cp(sb2.at[1, :, r, w], rz1.at[1, :, r, w], 1, zm)]
        direct = [cp(sdm.at[:, r, w], rzd.at[0, :, r, w], 3, zm), cp(sd1.at[:, r, w], rzd.at[1, :, r, w], 2, zp)]
        second = [cp(rz1.at[0, :, r, w], rz2.at[0, :, r, w], 4, zp), cp(rz1.at[1, :, r, w], rz2.at[1, :, r, w], 5, zm)]
        return first, direct, second

    def mlp(c, g):
        r, R = rows[c], SIZES[c]
        if g == 0:
            for k in range(8):
                blk = xn.at[held[k], 1 - core, r, :]
                rcopy(blk, blk, (k_s, k_r), (c, k), sib).wait_recv()
        if c == 0:
            for cp in lw[g]:
                cp.wait()
        base, tile = 2 * span[g][0], 2 * (span[g][1] - span[g][0]) // SPLIT

        @pl.loop(0, SPLIT)
        def _(j):
            cols = pl.ds(pl.multiple_of(base + j * tile, 128), tile)
            a = jnp.concatenate(
                [xn[pl.ds(b * 2, 2), :, r, :].reshape(4 * R, 2048) for b in (op2, up1, dn1, z)], axis=0)
            p = jnp.dot(a, wgu[:, cols], preferred_element_type=F32).reshape(4, 2, 2, R, tile)
            sb2[:, :, r, cols] = p[0].astype(BF16)
            sp1[:, r, cols] = p[1, 0]
            sd1[:, r, cols] = p[1, 1].astype(BF16)
            sdm[:, r, cols] = p[2, 0].astype(BF16)
            spm[:, r, cols] = p[2, 1]
            own[:, :, r, cols] = p[3]
        first, direct, _ = zsteps(c, g)
        for cp in first + direct:
            go(cp)

    def z2(c, g):
        first, _, second = zsteps(c, g)
        r, w = rows[c], gcols[g]
        for h, part in ((0, sp1), (1, spm)):
            first[h].wait_recv()
            for j in range(2):
                rz1[h, j, r, w] = (rz1[h, j, r, w].astype(F32) + part[j, r, w]).astype(BF16)
            go(second[h])

    def vcopy(c, g):
        return rcopy(sy.at[:, rows[c], gcols[g]], ryz.at[:, rows[c], gcols[g]], (v_s, v_r), (c, g), at(yhi=1 - yhi))

    def z3(c, g):
        _, direct, second = zsteps(c, g)
        for cp in direct + second:
            cp.wait_recv()
        r, w, h = rows[c], gcols[g], 1 - yhi
        for j in range(2):
            sy[j, r, w] = (own[h, j, r, w] + rz2[h, j, r, w].astype(F32) + rzd[h, j, r, w].astype(F32)).astype(BF16)
        go(vcopy(c, g))

    def out(c, g):
        vcopy(c, g).wait_recv()
        r, (a, b) = rows[c], span[g]
        for j in range(2):
            def total(o):
                w = pl.ds(2 * a + o * (b - a), b - a)
                return (own[yhi, j, r, w] + rz2[yhi, j, r, w].astype(F32)
                        + rzd[yhi, j, r, w].astype(F32) + ryz[j, r, w].astype(F32))
            v, u = total(0), total(1)
            hid[j, r, pl.ds(a, b - a)] = v / (1.0 + jnp.exp(-v)) * u
        cp = pltpu.make_async_copy(hid.at[:, r, pl.ds(a, b - a)], hid_h.at[:, r, pl.ds(a, b - a)], st.at[1 + g, c])
        cp.start()
        outs.append(cp)

    outs = []
    def grouped(f):
        return [functools.partial(f, g=0), functools.partial(f, g=1)]
    stage = [s_heads, s_proj, s_pair, s_x2, s_x3, s_res, s_norm, s_g2, s_g3, s_gath,
             *grouped(mlp), *grouped(z2), *grouped(z3), *grouped(out)]
    for s, c in ORDER:
        stage[s](c)
    for cp in sends:
        cp.make().wait_send()
    for cp in outs:
        cp.wait()


def handover(res_h, hid_h, res_o, hid_o, res_v, hid_v, sem):
    def moves(way, src, dst, k):
        n = src.shape[0] // HAND
        return [pltpu.make_async_copy(src.at[pl.ds(i * n, n)], dst.at[pl.ds(i * n, n)], sem.at[way, k, i])
                for i in range(HAND)]
    into = moves(0, res_h, res_v, 0) + moves(0, hid_h, hid_v, 1)
    back = moves(1, res_v, res_o, 0) + moves(1, hid_v, hid_o, 1)
    for cp in into:
        cp.start()
    for cp, nx in zip(into, back):
        cp.wait()
        nx.start()
    for cp in back:
        cp.wait()


def on_device(heads_output, residual_in, out_weight, norm_gain, gate_weight, up_weight):
    C = len(SIZES)
    dm, ffd = gate_weight.shape
    rows = residual_in.shape[0]
    anys = pl.BlockSpec(memory_space=pl.ANY)
    vm = pl.BlockSpec(memory_space=pltpu.VMEM)
    dma = pltpu.SemaphoreType.DMA
    V = pltpu.VMEM
    zb, zh = (2, 2, rows, 2 * ffd), (2, rows, 2 * ffd)
    res, hid = pl.pallas_call(
        functools.partial(body, C),
        out_shape=(jax.ShapeDtypeStruct((rows, dm), F32), jax.ShapeDtypeStruct((2, rows, ffd), F32)),
        in_specs=[anys, anys, anys, vm, anys, anys],
        out_specs=(anys, anys),
        scratch_shapes=[
            V((8, 2, rows, 512), BF16), V((512, dm), BF16), V((dm, 2 * ffd), BF16), V((rows, dm), BF16),
            V((8, rows, dm), F32), V((8, rows, dm), F32), V((8, rows, dm), F32),
            V((2, rows, dm), F32), V((2, rows, dm), F32), V((2, rows, dm), F32), V((rows, dm), F32),
            V((rows, dm), F32), V((8, rows, 128), F32), V((8, 2, rows, dm), BF16),
            V(zb, BF16), V(zh, BF16), V(zh, BF16), V(zh, F32), V(zh, F32), V(zb, F32), V(zb, BF16), V(zb, BF16), V(zb, BF16),
            V((2, rows, 2 * ffd), BF16), V((2, rows, 2 * ffd), BF16), V((2, rows, ffd), F32),
            dma((7,)), dma((3, C)), dma((C, 7)), dma((C, 7)), dma((C,)), dma((C,)), dma((C, 6)), dma((C, 6)),
            dma((C,)), dma((C,)), dma((C, 7)), dma((C, 7)), dma((C, 7)), dma((C, 7)), dma((C, 8)), dma((C, 8)),
            dma((C, 2, 6)), dma((C, 2, 6)), dma((C, 2)), dma((C, 2)),
        ],
        compiler_params=pltpu.CompilerParams(collective_id=0, has_side_effects=True, vmem_limit_bytes=62 << 20),
        name="layer",
    )(heads_output.reshape(2, rows, 512), residual_in, out_weight, norm_gain.reshape(1, dm), gate_weight, up_weight)
    out = (jax.ShapeDtypeStruct(res.shape, F32), jax.ShapeDtypeStruct((2 * rows, ffd), F32))
    return pl.pallas_call(
        handover, out_shape=out, in_specs=[anys, anys], out_specs=(anys, anys),
        scratch_shapes=[V(res.shape, F32), V((2 * rows, ffd), F32), dma((2, 2, HAND))], name="handover",
    )(res, hid.reshape(2 * rows, ffd))


def solution(mesh):
    return jax.shard_map(
        on_device, mesh=mesh,
        in_specs=(P("narrow", "wide"), P("wide", "narrow"), P("wide", "narrow"), P("narrow"),
                  P("narrow", "wide"), P("narrow", "wide")),
        out_specs=(P("wide", "narrow"), P("narrow", "wide")), check_vma=False)
```

```python
import functools

import jax
import jax.numpy as jnp
from jax import lax
from jax.experimental import pallas as pl
from jax.experimental.pallas import tpu as pltpu
from jax.sharding import PartitionSpec as P

D = 16384
MESH = pl.DeviceIdType.MESH
F32, BF16 = jnp.float32, jnp.bfloat16
SIZES = (8, 8, 16, 16, 8, 8)
DIRECT = (True, False, False, False, False, False)
PT = 1024
SPLIT = 1
HAND = 2


ORDER = [
    (0, 0), (0, 1), (0, 2), (0, 3), (1, 0), (1, 1), (0, 5), (2, 0), (2, 1), (3, 0), (1, 2), (3, 1), (0, 4), (2, 2),
    (4, 1), (4, 0), (1, 3), (3, 2), (2, 3), (5, 1), (5, 0), (1, 4), (6, 1), (4, 2), (3, 3), (7, 1), (1, 5), (8, 1),
    (6, 0), (5, 2), (4, 3), (9, 1), (2, 4), (6, 2), (10, 1), (7, 0), (8, 0), (11, 1), (9, 0), (3, 4), (5, 3),
    (10, 0), (7, 2), (8, 2), (2, 5), (11, 0), (6, 3), (4, 4), (12, 1), (9, 2), (12, 0), (3, 5), (13, 0), (13, 1),
    (10, 2), (7, 3), (8, 3), (5, 4), (11, 2), (4, 5), (12, 2), (14, 1), (9, 3), (5, 5), (13, 2), (6, 4), (10, 3),
    (14, 0), (11, 3), (14, 2), (7, 4), (8, 4), (6, 5), (9, 4), (7, 5), (8, 5), (12, 3), (15, 2), (15, 0), (13, 3),
    (16, 2), (9, 5), (10, 4), (15, 1), (10, 5), (14, 3), (11, 5), (12, 5), (11, 4), (16, 1), (12, 4), (17, 1),
    (15, 3), (13, 5), (13, 4), (14, 5), (14, 4), (15, 5), (16, 3), (15, 4), (16, 0), (16, 5), (17, 3), (16, 4),
    (17, 0), (17, 2), (17, 5), (17, 4),
]


def body(C, heads_h, rin_h, wo_h, gain_ref, wg_h, wu_h, res_h, hid_h,
         heads, wo, wgu, rin, s2, acc, r2, rx1, rx2, rxd, ry, res, sq, xn,
         sb2, sd1, sdm, sp1, spm, own, rz1, rz2, rzd, sy, ryz, hid,
         ld, st, h_s, h_r, c_s, c_r, x_s, x_r, y_s, y_r, q_s, q_r, g_s, g_r, k_s, k_r,
         z_s, z_r, v_s, v_r):
    ff = wgu.shape[1]
    half = ff // 2
    wide = lax.axis_index("wide")
    narrow = lax.axis_index("narrow")
    ylo, x, core = wide // 8, (wide // 2) % 4, wide % 2
    z, yhi = narrow // 2, narrow % 2
    up1, dn1, op2 = (z + 1) % 4, (z + 3) % 4, (z + 2) % 4

    def at(ylo=ylo, x=x, core=core, z=z, yhi=yhi):
        return (ylo * 8 + x * 2 + core, z * 2 + yhi)

    nar = []
    for dz in range(4):
        for dy in range(2):
            if dz or dy:
                nar.append((at(z=(z + dz) % 4, yhi=(yhi + dy) % 2), ((z + 4 - dz) % 4) * 2 + (yhi + dy) % 2))
    sib = at(core=1 - core)

    sends, got, met = [], set(), set()

    def first_time(s):
        new = s not in met
        met.add(s)
        return new

    class rcopy:
        def __init__(self, src, dst, sems, idx, dev, ridx=None):
            self.key = (id(sems[0]),) + idx
            self.make = lambda: pltpu.make_async_remote_copy(
                src_ref=src, dst_ref=dst, send_sem=sems[0].at[idx], recv_sem=sems[1].at[idx if ridx is None else ridx],
                device_id=dev, device_id_type=MESH)

        def wait_recv(self):
            got.add(self.key)
            self.make().wait_recv()

    def go(cp):
        cp.make().start()
        sends.append(cp)

    lh = pltpu.make_async_copy(heads_h, heads.at[narrow], ld.at[0])
    lo = pltpu.make_async_copy(wo_h, wo, ld.at[1])
    lr = pltpu.make_async_copy(rin_h, rin, ld.at[2])
    cut = half // 256 * 128 + 128
    span = ((0, cut), (cut, half))
    gcols = [pl.ds(2 * a, 2 * (b - a)) for a, b in span]
    lw = []
    for g, (a, b) in enumerate(span):
        lw.append([pltpu.make_async_copy(w.at[:, pl.ds(a, b - a)], wgu.at[:, pl.ds(2 * a + o * (b - a), b - a)],
                                         ld.at[3 + 2 * g + o]) for o, w in enumerate((wg_h, wu_h))])
    for cp in [lh, lo]:
        cp.start()

    bar = pltpu.get_barrier_semaphore()
    peers = [t for t, _ in nar] + [at(x=(x + dx) % 4, ylo=yy) for dx in (1, 2, 3) for yy in (ylo, 1 - ylo)] + [at(ylo=1 - ylo), sib]
    for t in peers:
        pl.semaphore_signal(bar, inc=1, device_id=t, device_id_type=MESH)
    pl.semaphore_wait(bar, len(peers))

    lh.wait()
    rows = [pl.ds(sum(SIZES[:c]), SIZES[c]) for c in range(C)]
    mine = ylo * 4 + x

    def s_heads(c):
        for i, (t, _) in enumerate(nar):
            blk = heads.at[narrow, :, rows[c], :]
            go(rcopy(blk, blk, (h_s, h_r), (c, i,), t))

    def s_proj(c):
        for i, (t, src) in enumerate(nar):
            blk = heads.at[src, :, rows[c], :]
            rcopy(blk, blk, (h_s, h_r), (c, i,), t).wait_recv()
        if first_time(1):
            lo.wait()
            for cp in [lr] + lw[0] + lw[1]:
                cp.start()

        @pl.loop(0, 2048 // PT)
        def _(j):
            cols = pl.ds(pl.multiple_of(j * PT, PT), PT)
            a = jnp.concatenate([heads[:, p, rows[c], :].reshape(8 * SIZES[c], 512) for p in (1 - core, core)], axis=0)
            p = jnp.dot(a, wo[:, cols], preferred_element_type=F32)
            s2[:, rows[c], cols] = p[:8 * SIZES[c]].reshape(8, SIZES[c], PT)
            acc[:, rows[c], cols] = p[8 * SIZES[c]:].reshape(8, SIZES[c], PT)
        go(rcopy(s2.at[:, rows[c], :], r2.at[:, rows[c], :], (c_s, c_r), (c,), sib))

    def xsteps(c):
        xp, xm = at(x=(x + 1) % 4), at(x=(x + 3) % 4)
        far, nx, pv = (x + 2) % 4, (x + 1) % 4, (x + 3) % 4
        r = rows[c]
        first = [rcopy(acc.at[far, r, :], rx1.at[0, r, :], (x_s, x_r), (c, 0,), xp),
                 rcopy(acc.at[4 + far, r, :], rx1.at[1, r, :], (x_s, x_r), (c, 1,), xm)]
        direct = [rcopy(acc.at[4 + nx, r, :], rxd.at[1, r, :], (x_s, x_r), (c, 2,), xp),
                  rcopy(acc.at[pv, r, :], rxd.at[0, r, :], (x_s, x_r), (c, 3,), xm)]
        second = [rcopy(rx1.at[0, r, :], rx2.at[0, r, :], (x_s, x_r), (c, 4,), xp),
                  rcopy(rx1.at[1, r, :], rx2.at[1, r, :], (x_s, x_r), (c, 5,), xm)]
        return first, direct, second, (nx, 4 + pv)

    def s_pair(c):
        rcopy(s2.at[:, rows[c], :], r2.at[:, rows[c], :], (c_s, c_r), (c,), sib).wait_recv()

        @pl.loop(0, 8)
        def _(b):
            acc[b, rows[c], :] = acc[b, rows[c], :] + r2[b, rows[c], :]
        first, direct, _, _ = xsteps(c)
        for cp in first + direct:
            go(cp)

    def s_x2(c):
        first, _, second, mid = xsteps(c)
        for h in range(2):
            first[h].wait_recv()
            rx1[h, rows[c], :] = rx1[h, rows[c], :] + acc[mid[h], rows[c], :]
            go(second[h])

    def ycopy(c):
        return rcopy(acc.at[(1 - ylo) * 4 + x, rows[c], :], ry.at[rows[c], :], (y_s, y_r), (c,), at(ylo=1 - ylo))

    def s_x3(c):
        _, direct, second, _ = xsteps(c)
        for cp in direct + second:
            cp.wait_recv()
        r = rows[c]
        for h in (1 - ylo, ylo):
            b = h * 4 + x
            acc[b, r, :] = acc[b, r, :] + rx2[h, r, :] + rxd[h, r, :]
            if h is not ylo:
                go(ycopy(c))

    def s_res(c):
        ycopy(c).wait_recv()
        if first_time(5):
            lr.wait()
        r = rows[c]
        total = acc[mine, r, :] + ry[r, :]
        total = rin[r, :].astype(F32) + total
        res[r, :] = total
        out = pltpu.make_async_copy(res.at[r, :], res_h.at[r, :], st.at[0, c])
        out.start()
        outs.append(out)
        sq[narrow, r, :] = jnp.broadcast_to(jnp.sum(total * total, axis=1, keepdims=True), (SIZES[c], 128))
        for i, (t, _) in enumerate(nar):
            blk = sq.at[narrow, r, :]
            go(rcopy(blk, blk, (q_s, q_r), (c, i,), t))

    def s_norm(c):
        r = rows[c]
        for i, (t, src) in enumerate(nar):
            blk = sq.at[src, r, :]
            rcopy(blk, blk, (q_s, q_r), (c, i,), t).wait_recv()
        ssum = sq[0, r, :]
        for i in range(1, 8):
            ssum = ssum + sq[i, r, :]
        scale = (1.0 / jnp.sqrt(ssum / D + 1e-05))[:, :1]
        xn[mine, core, r, :] = (res[r, :] * scale * gain_ref[...]).astype(BF16)
        for i, t in ((0, xp), (1, xm), (2, yp)):
            go(gcopy(c, mine, i, t))
        other = 1 - ylo
        go(gcopy(c, mine, 3, at(x=nxx, ylo=other)))
        go(gcopy(c, mine, 4, at(x=pvx, ylo=other)))
        if DIRECT[c]:
            go(gcopy(c, mine, 5, at(x=far), 5 + ylo))
            go(gcopy(c, mine, 6, at(x=far, ylo=other), 5 + ylo))
        go(kcopy(c, 0, mine))

    xp, xm, yp = at(x=(x + 1) % 4), at(x=(x + 3) % 4), at(ylo=1 - ylo)
    yours = (1 - ylo) * 4 + x

    def gcopy(c, b, i, t, ri=None):
        blk = xn.at[b, core, rows[c], :]
        return rcopy(blk, blk, (g_s, g_r), (c, i), t, None if ri is None else (c, ri))

    def kcopy(c, i, b):
        blk = xn.at[b, core, rows[c], :]
        return rcopy(blk, blk, (k_s, k_r), (c, i), sib)

    pvx, nxx, far = (x + 3) % 4, (x + 1) % 4, (x + 2) % 4
    held = [mine, ylo * 4 + pvx, ylo * 4 + nxx, yours, (1 - ylo) * 4 + pvx, (1 - ylo) * 4 + nxx, far, 4 + far]

    def s_g2(c):
        gcopy(c, yours, 2, yp).wait_recv()
        go(kcopy(c, 3, yours))

    def s_g3(c):
        gcopy(c, held[1], 0, xp).wait_recv()
        gcopy(c, held[2], 1, xm).wait_recv()
        gcopy(c, held[4], 3, xp).wait_recv()
        gcopy(c, held[5], 4, xm).wait_recv()
        if not DIRECT[c]:
            go(gcopy(c, pvx, 5, xp))
            go(gcopy(c, 4 + nxx, 6, xm))
        for k in (1, 2, 4, 5):
            go(kcopy(c, k, held[k]))

    def s_gath(c):
        gcopy(c, far, 5, xp).wait_recv()
        gcopy(c, 4 + far, 6, xm).wait_recv()
        for k in (6, 7):
            go(kcopy(c, k, held[k]))

    zp, zm = at(z=up1), at(z=dn1)

    def zsteps(c, g):
        r, w = rows[c], gcols[g]

        def cp(src, dst, i, t):
            return rcopy(src, dst, (z_s, z_r), (c, g, i), t)
        first = [cp(sb2.at[0, :, r, w], rz1.at[0, :, r, w], 0, zp), cp(sb2.at[1, :, r, w], rz1.at[1, :, r, w], 1, zm)]
        direct = [cp(sdm.at[:, r, w], rzd.at[0, :, r, w], 3, zm), cp(sd1.at[:, r, w], rzd.at[1, :, r, w], 2, zp)]
        second = [cp(rz1.at[0, :, r, w], rz2.at[0, :, r, w], 4, zp), cp(rz1.at[1, :, r, w], rz2.at[1, :, r, w], 5, zm)]
        return first, direct, second

    def mlp(c, g):
        r, R = rows[c], SIZES[c]
        if g == 0:
            for k in range(8):
                blk = xn.at[held[k], 1 - core, r, :]
                rcopy(blk, blk, (k_s, k_r), (c, k), sib).wait_recv()
        if first_time(10 + g):
            for cp in lw[g]:
                cp.wait()
        base, tile = 2 * span[g][0], 2 * (span[g][1] - span[g][0]) // SPLIT

        @pl.loop(0, SPLIT)
        def _(j):
            cols = pl.ds(pl.multiple_of(base + j * tile, 128), tile)
            a = jnp.concatenate(
                [xn[pl.ds(b * 2, 2), :, r, :].reshape(4 * R, 2048) for b in (op2, up1, dn1, z)], axis=0)
            p = jnp.dot(a, wgu[:, cols], preferred_element_type=F32).reshape(4, 2, 2, R, tile)
            sb2[:, :, r, cols] = p[0].astype(BF16)
            sp1[:, r, cols] = p[1, 0]
            sd1[:, r, cols] = p[1, 1].astype(BF16)
            sdm[:, r, cols] = p[2, 0].astype(BF16)
            spm[:, r, cols] = p[2, 1]
            own[:, :, r, cols] = p[3]
        first, direct, _ = zsteps(c, g)
        for cp in first + direct:
            go(cp)

    def z2(c, g):
        first, _, second = zsteps(c, g)
        r, w = rows[c], gcols[g]
        for h, part in ((0, sp1), (1, spm)):
            first[h].wait_recv()
            for j in range(2):
                rz1[h, j, r, w] = (rz1[h, j, r, w].astype(F32) + part[j, r, w]).astype(BF16)
            go(second[h])

    def vcopy(c, g):
        return rcopy(sy.at[:, rows[c], gcols[g]], ryz.at[:, rows[c], gcols[g]], (v_s, v_r), (c, g), at(yhi=1 - yhi))

    def z3(c, g):
        _, direct, second = zsteps(c, g)
        for cp in direct + second:
            cp.wait_recv()
        r, w, h = rows[c], gcols[g], 1 - yhi
        for j in range(2):
            sy[j, r, w] = (own[h, j, r, w] + rz2[h, j, r, w].astype(F32) + rzd[h, j, r, w].astype(F32)).astype(BF16)
        go(vcopy(c, g))

    def out(c, g):
        vcopy(c, g).wait_recv()
        r, (a, b) = rows[c], span[g]
        for j in range(2):
            def total(o):
                w = pl.ds(2 * a + o * (b - a), b - a)
                return (own[yhi, j, r, w] + rz2[yhi, j, r, w].astype(F32)
                        + rzd[yhi, j, r, w].astype(F32) + ryz[j, r, w].astype(F32))
            v, u = total(0), total(1)
            hid[j, r, pl.ds(a, b - a)] = v / (1.0 + jnp.exp(-v)) * u
        cp = pltpu.make_async_copy(hid.at[:, r, pl.ds(a, b - a)], hid_h.at[:, r, pl.ds(a, b - a)], st.at[1 + g, c])
        cp.start()
        outs.append(cp)

    outs = []
    def grouped(f):
        return [functools.partial(f, g=0), functools.partial(f, g=1)]
    stage = [s_heads, s_proj, s_pair, s_x2, s_x3, s_res, s_norm, s_g2, s_g3, s_gath,
             *grouped(mlp), *grouped(z2), *grouped(z3), *grouped(out)]
    for s, c in ORDER:
        stage[s](c)
    for cp in sends:
        cp.make().wait_send()
    for cp in outs:
        cp.wait()


def handover(res_h, hid_h, res_o, hid_o, res_v, hid_v, sem):
    def moves(way, src, dst, k):
        n = src.shape[0] // HAND
        return [pltpu.make_async_copy(src.at[pl.ds(i * n, n)], dst.at[pl.ds(i * n, n)], sem.at[way, k, i])
                for i in range(HAND)]
    into = moves(0, res_h, res_v, 0) + moves(0, hid_h, hid_v, 1)
    back = moves(1, res_v, res_o, 0) + moves(1, hid_v, hid_o, 1)
    for cp in into:
        cp.start()
    for cp, nx in zip(into, back):
        cp.wait()
        nx.start()
    for cp in back:
        cp.wait()


def on_device(heads_output, residual_in, out_weight, norm_gain, gate_weight, up_weight):
    C = len(SIZES)
    dm, ffd = gate_weight.shape
    rows = residual_in.shape[0]
    anys = pl.BlockSpec(memory_space=pl.ANY)
    vm = pl.BlockSpec(memory_space=pltpu.VMEM)
    dma = pltpu.SemaphoreType.DMA
    V = pltpu.VMEM
    zb, zh = (2, 2, rows, 2 * ffd), (2, rows, 2 * ffd)
    res, hid = pl.pallas_call(
        functools.partial(body, C),
        out_shape=(jax.ShapeDtypeStruct((rows, dm), F32), jax.ShapeDtypeStruct((2, rows, ffd), F32)),
        in_specs=[anys, anys, anys, vm, anys, anys],
        out_specs=(anys, anys),
        scratch_shapes=[
            V((8, 2, rows, 512), BF16), V((512, dm), BF16), V((dm, 2 * ffd), BF16), V((rows, dm), BF16),
            V((8, rows, dm), F32), V((8, rows, dm), F32), V((8, rows, dm), F32),
            V((2, rows, dm), F32), V((2, rows, dm), F32), V((2, rows, dm), F32), V((rows, dm), F32),
            V((rows, dm), F32), V((8, rows, 128), F32), V((8, 2, rows, dm), BF16),
            V(zb, BF16), V(zh, BF16), V(zh, BF16), V(zh, F32), V(zh, F32), V(zb, F32), V(zb, BF16), V(zb, BF16), V(zb, BF16),
            V((2, rows, 2 * ffd), BF16), V((2, rows, 2 * ffd), BF16), V((2, rows, ffd), F32),
            dma((7,)), dma((3, C)), dma((C, 7)), dma((C, 7)), dma((C,)), dma((C,)), dma((C, 6)), dma((C, 6)),
            dma((C,)), dma((C,)), dma((C, 7)), dma((C, 7)), dma((C, 7)), dma((C, 7)), dma((C, 8)), dma((C, 8)),
            dma((C, 2, 6)), dma((C, 2, 6)), dma((C, 2)), dma((C, 2)),
        ],
        compiler_params=pltpu.CompilerParams(collective_id=0, has_side_effects=True, vmem_limit_bytes=62 << 20),
        name="layer",
    )(heads_output.reshape(2, rows, 512), residual_in, out_weight, norm_gain.reshape(1, dm), gate_weight, up_weight)
    out = (jax.ShapeDtypeStruct(res.shape, F32), jax.ShapeDtypeStruct((2 * rows, ffd), F32))
    return pl.pallas_call(
        handover, out_shape=out, in_specs=[anys, anys], out_specs=(anys, anys),
        scratch_shapes=[V(res.shape, F32), V((2 * rows, ffd), F32), dma((2, 2, HAND))], name="handover",
    )(res, hid.reshape(2 * rows, ffd))


def solution(mesh):
    return jax.shard_map(
        on_device, mesh=mesh,
        in_specs=(P("narrow", "wide"), P("wide", "narrow"), P("wide", "narrow"), P("narrow"),
                  P("narrow", "wide"), P("narrow", "wide")),
        out_specs=(P("wide", "narrow"), P("narrow", "wide")), check_vma=False)
```

```python
import functools

import jax
import jax.numpy as jnp
from jax import lax
from jax.experimental import pallas as pl
from jax.experimental.pallas import tpu as pltpu
from jax.sharding import PartitionSpec as P

D = 16384
MESH = pl.DeviceIdType.MESH
F32, BF16 = jnp.float32, jnp.bfloat16
SIZES = (8, 8, 16, 16, 8, 8)
DIRECT = (True, False, False, False, False, False)
PT = 1024
SPLIT = 1
HAND = 2


ORDER = [
    (0, 0), (0, 1), (0, 5), (0, 2), (0, 3), (1, 0), (1, 1), (2, 0), (2, 1), (1, 5), (1, 2), (3, 0), (1, 3), (2, 2),
    (0, 4), (4, 0), (3, 1), (3, 2), (5, 0), (2, 3), (4, 1), (6, 0), (4, 2), (5, 1), (7, 0), (3, 3), (6, 1), (2, 5),
    (8, 0), (5, 2), (1, 4), (4, 3), (7, 1), (8, 1), (9, 0), (6, 2), (3, 5), (2, 4), (10, 0), (5, 3), (9, 1),
    (11, 0), (10, 1), (7, 2), (8, 2), (4, 5), (11, 1), (6, 3), (12, 1), (9, 2), (3, 4), (12, 0), (5, 5), (13, 1),
    (13, 0), (10, 2), (7, 3), (8, 3), (14, 1), (4, 4), (11, 2), (9, 3), (5, 4), (6, 5), (14, 0), (12, 2), (15, 0),
    (10, 3), (6, 4), (11, 3), (7, 4), (7, 5), (12, 3), (8, 5), (8, 4), (13, 2), (13, 3), (15, 1), (9, 5), (9, 4),
    (14, 2), (16, 1), (10, 4), (10, 5), (11, 5), (15, 2), (11, 4), (12, 4), (14, 3), (15, 3), (12, 5), (17, 1),
    (13, 4), (13, 5), (16, 3), (16, 0), (14, 4), (17, 0), (14, 5), (16, 2), (15, 4), (17, 2), (15, 5), (16, 5),
    (16, 4), (17, 3), (17, 4), (17, 5),
]


def body(C, heads_h, rin_h, wo_h, gain_ref, wg_h, wu_h, res_h, hid_h,
         heads, wo, wgu, rin, s2, acc, r2, rx1, rx2, rxd, ry, res, sq, xn,
         sb2, sd1, sdm, sp1, spm, own, rz1, rz2, rzd, sy, ryz, hid,
         ld, st, h_s, h_r, c_s, c_r, x_s, x_r, y_s, y_r, q_s, q_r, g_s, g_r, k_s, k_r,
         z_s, z_r, v_s, v_r):
    ff = wgu.shape[1]
    half = ff // 2
    wide = lax.axis_index("wide")
    narrow = lax.axis_index("narrow")
    ylo, x, core = wide // 8, (wide // 2) % 4, wide % 2
    z, yhi = narrow // 2, narrow % 2
    up1, dn1, op2 = (z + 1) % 4, (z + 3) % 4, (z + 2) % 4

    def at(ylo=ylo, x=x, core=core, z=z, yhi=yhi):
        return (ylo * 8 + x * 2 + core, z * 2 + yhi)

    nar = []
    for dz in range(4):
        for dy in range(2):
            if dz or dy:
                nar.append((at(z=(z + dz) % 4, yhi=(yhi + dy) % 2), ((z + 4 - dz) % 4) * 2 + (yhi + dy) % 2))
    sib = at(core=1 - core)

    sends, got, met = [], set(), set()

    def first_time(s):
        new = s not in met
        met.add(s)
        return new

    class rcopy:
        def __init__(self, src, dst, sems, idx, dev, ridx=None):
            self.key = (id(sems[0]),) + idx
            self.make = lambda: pltpu.make_async_remote_copy(
                src_ref=src, dst_ref=dst, send_sem=sems[0].at[idx], recv_sem=sems[1].at[idx if ridx is None else ridx],
                device_id=dev, device_id_type=MESH)

        def wait_recv(self):
            got.add(self.key)
            self.make().wait_recv()

    def go(cp):
        cp.make().start()
        sends.append(cp)

    lh = pltpu.make_async_copy(heads_h, heads.at[narrow], ld.at[0])
    lo = pltpu.make_async_copy(wo_h, wo, ld.at[1])
    lr = pltpu.make_async_copy(rin_h, rin, ld.at[2])
    cut = half // 256 * 128 + 128
    span = ((0, cut), (cut, half))
    gcols = [pl.ds(2 * a, 2 * (b - a)) for a, b in span]
    lw = []
    for g, (a, b) in enumerate(span):
        lw.append([pltpu.make_async_copy(w.at[:, pl.ds(a, b - a)], wgu.at[:, pl.ds(2 * a + o * (b - a), b - a)],
                                         ld.at[3 + 2 * g + o]) for o, w in enumerate((wg_h, wu_h))])
    for cp in [lh, lo]:
        cp.start()

    bar = pltpu.get_barrier_semaphore()
    peers = [t for t, _ in nar] + [at(x=(x + dx) % 4, ylo=yy) for dx in (1, 2, 3) for yy in (ylo, 1 - ylo)] + [at(ylo=1 - ylo), sib]
    for t in peers:
        pl.semaphore_signal(bar, inc=1, device_id=t, device_id_type=MESH)
    pl.semaphore_wait(bar, len(peers))

    lh.wait()
    rows = [pl.ds(sum(SIZES[:c]), SIZES[c]) for c in range(C)]
    mine = ylo * 4 + x

    def s_heads(c):
        for i, (t, _) in enumerate(nar):
            blk = heads.at[narrow, :, rows[c], :]
            go(rcopy(blk, blk, (h_s, h_r), (c, i,), t))

    def s_proj(c):
        for i, (t, src) in enumerate(nar):
            blk = heads.at[src, :, rows[c], :]
            rcopy(blk, blk, (h_s, h_r), (c, i,), t).wait_recv()
        if first_time(1):
            lo.wait()
            for cp in [lr] + lw[0] + lw[1]:
                cp.start()

        @pl.loop(0, 2048 // PT)
        def _(j):
            cols = pl.ds(pl.multiple_of(j * PT, PT), PT)
            a = jnp.concatenate([heads[:, p, rows[c], :].reshape(8 * SIZES[c], 512) for p in (1 - core, core)], axis=0)
            p = jnp.dot(a, wo[:, cols], preferred_element_type=F32)
            s2[:, rows[c], cols] = p[:8 * SIZES[c]].reshape(8, SIZES[c], PT)
            acc[:, rows[c], cols] = p[8 * SIZES[c]:].reshape(8, SIZES[c], PT)
        go(rcopy(s2.at[:, rows[c], :], r2.at[:, rows[c], :], (c_s, c_r), (c,), sib))

    def xsteps(c):
        xp, xm = at(x=(x + 1) % 4), at(x=(x + 3) % 4)
        far, nx, pv = (x + 2) % 4, (x + 1) % 4, (x + 3) % 4
        r = rows[c]
        first = [rcopy(acc.at[far, r, :], rx1.at[0, r, :], (x_s, x_r), (c, 0,), xp),
                 rcopy(acc.at[4 + far, r, :], rx1.at[1, r, :], (x_s, x_r), (c, 1,), xm)]
        direct = [rcopy(acc.at[4 + nx, r, :], rxd.at[1, r, :], (x_s, x_r), (c, 2,), xp),
                  rcopy(acc.at[pv, r, :], rxd.at[0, r, :], (x_s, x_r), (c, 3,), xm)]
        second = [rcopy(rx1.at[0, r, :], rx2.at[0, r, :], (x_s, x_r), (c, 4,), xp),
                  rcopy(rx1.at[1, r, :], rx2.at[1, r, :], (x_s, x_r), (c, 5,), xm)]
        return first, direct, second, (nx, 4 + pv)

    def s_pair(c):
        rcopy(s2.at[:, rows[c], :], r2.at[:, rows[c], :], (c_s, c_r), (c,), sib).wait_recv()

        @pl.loop(0, 8)
        def _(b):
            acc[b, rows[c], :] = acc[b, rows[c], :] + r2[b, rows[c], :]
        first, direct, _, _ = xsteps(c)
        for cp in first + direct:
            go(cp)

    def s_x2(c):
        first, _, second, mid = xsteps(c)
        for h in range(2):
            first[h].wait_recv()
            rx1[h, rows[c], :] = rx1[h, rows[c], :] + acc[mid[h], rows[c], :]
            go(second[h])

    def ycopy(c):
        return rcopy(acc.at[(1 - ylo) * 4 + x, rows[c], :], ry.at[rows[c], :], (y_s, y_r), (c,), at(ylo=1 - ylo))

    def s_x3(c):
        _, direct, second, _ = xsteps(c)
        for cp in direct + second:
            cp.wait_recv()
        r = rows[c]
        for h in (1 - ylo, ylo):
            b = h * 4 + x
            acc[b, r, :] = acc[b, r, :] + rx2[h, r, :] + rxd[h, r, :]
            if h is not ylo:
                go(ycopy(c))

    def s_res(c):
        ycopy(c).wait_recv()
        if first_time(5):
            lr.wait()
        r = rows[c]
        total = acc[mine, r, :] + ry[r, :]
        total = rin[r, :].astype(F32) + total
        res[r, :] = total
        out = pltpu.make_async_copy(res.at[r, :], res_h.at[r, :], st.at[0, c])
        out.start()
        outs.append(out)
        sq[narrow, r, :] = jnp.broadcast_to(jnp.sum(total * total, axis=1, keepdims=True), (SIZES[c], 128))
        for i, (t, _) in enumerate(nar):
            blk = sq.at[narrow, r, :]
            go(rcopy(blk, blk, (q_s, q_r), (c, i,), t))

    def s_norm(c):
        r = rows[c]
        for i, (t, src) in enumerate(nar):
            blk = sq.at[src, r, :]
            rcopy(blk, blk, (q_s, q_r), (c, i,), t).wait_recv()
        ssum = sq[0, r, :]
        for i in range(1, 8):
            ssum = ssum + sq[i, r, :]
        scale = (1.0 / jnp.sqrt(ssum / D + 1e-05))[:, :1]
        xn[mine, core, r, :] = (res[r, :] * scale * gain_ref[...]).astype(BF16)
        for i, t in ((0, xp), (1, xm), (2, yp)):
            go(gcopy(c, mine, i, t))
        other = 1 - ylo
        go(gcopy(c, mine, 3, at(x=nxx, ylo=other)))
        go(gcopy(c, mine, 4, at(x=pvx, ylo=other)))
        if DIRECT[c]:
            go(gcopy(c, mine, 5, at(x=far), 5 + ylo))
            go(gcopy(c, mine, 6, at(x=far, ylo=other), 5 + ylo))
        go(kcopy(c, 0, mine))

    xp, xm, yp = at(x=(x + 1) % 4), at(x=(x + 3) % 4), at(ylo=1 - ylo)
    yours = (1 - ylo) * 4 + x

    def gcopy(c, b, i, t, ri=None):
        blk = xn.at[b, core, rows[c], :]
        return rcopy(blk, blk, (g_s, g_r), (c, i), t, None if ri is None else (c, ri))

    def kcopy(c, i, b):
        blk = xn.at[b, core, rows[c], :]
        return rcopy(blk, blk, (k_s, k_r), (c, i), sib)

    pvx, nxx, far = (x + 3) % 4, (x + 1) % 4, (x + 2) % 4
    held = [mine, ylo * 4 + pvx, ylo * 4 + nxx, yours, (1 - ylo) * 4 + pvx, (1 - ylo) * 4 + nxx, far, 4 + far]

    def s_g2(c):
        gcopy(c, yours, 2, yp).wait_recv()
        go(kcopy(c, 3, yours))

    def s_g3(c):
        gcopy(c, held[1], 0, xp).wait_recv()
        gcopy(c, held[2], 1, xm).wait_recv()
        gcopy(c, held[4], 3, xp).wait_recv()
        gcopy(c, held[5], 4, xm).wait_recv()
        if not DIRECT[c]:
            go(gcopy(c, pvx, 5, xp))
            go(gcopy(c, 4 + nxx, 6, xm))
        for k in (1, 2, 4, 5):
            go(kcopy(c, k, held[k]))

    def s_gath(c):
        gcopy(c, far, 5, xp).wait_recv()
        gcopy(c, 4 + far, 6, xm).wait_recv()
        for k in (6, 7):
            go(kcopy(c, k, held[k]))

    zp, zm = at(z=up1), at(z=dn1)

    def zsteps(c, g):
        r, w = rows[c], gcols[g]

        def cp(src, dst, i, t):
            return rcopy(src, dst, (z_s, z_r), (c, g, i), t)
        first = [cp(sb2.at[0, :, r, w], rz1.at[0, :, r, w], 0, zp), cp(sb2.at[1, :, r, w], rz1.at[1, :, r, w], 1, zm)]
        direct = [cp(sdm.at[:, r, w], rzd.at[0, :, r, w], 3, zm), cp(sd1.at[:, r, w], rzd.at[1, :, r, w], 2, zp)]
        second = [cp(rz1.at[0, :, r, w], rz2.at[0, :, r, w], 4, zp), cp(rz1.at[1, :, r, w], rz2.at[1, :, r, w], 5, zm)]
        return first, direct, second

    def mlp(c, g):
        r, R = rows[c], SIZES[c]
        if g == 0:
            for k in range(8):
                blk = xn.at[held[k], 1 - core, r, :]
                rcopy(blk, blk, (k_s, k_r), (c, k), sib).wait_recv()
        if first_time(10 + g):
            for cp in lw[g]:
                cp.wait()
        base, tile = 2 * span[g][0], 2 * (span[g][1] - span[g][0]) // SPLIT

        @pl.loop(0, SPLIT)
        def _(j):
            cols = pl.ds(pl.multiple_of(base + j * tile, 128), tile)
            a = jnp.concatenate(
                [xn[pl.ds(b * 2, 2), :, r, :].reshape(4 * R, 2048) for b in (op2, up1, dn1, z)], axis=0)
            p = jnp.dot(a, wgu[:, cols], preferred_element_type=F32).reshape(4, 2, 2, R, tile)
            sb2[:, :, r, cols] = p[0].astype(BF16)
            sp1[:, r, cols] = p[1, 0]
            sd1[:, r, cols] = p[1, 1].astype(BF16)
            sdm[:, r, cols] = p[2, 0].astype(BF16)
            spm[:, r, cols] = p[2, 1]
            own[:, :, r, cols] = p[3]
        first, direct, _ = zsteps(c, g)
        for cp in first + direct:
            go(cp)

    def z2(c, g):
        first, _, second = zsteps(c, g)
        r, w = rows[c], gcols[g]
        for h, part in ((0, sp1), (1, spm)):
            first[h].wait_recv()
            for j in range(2):
                rz1[h, j, r, w] = (rz1[h, j, r, w].astype(F32) + part[j, r, w]).astype(BF16)
            go(second[h])

    def vcopy(c, g):
        return rcopy(sy.at[:, rows[c], gcols[g]], ryz.at[:, rows[c], gcols[g]], (v_s, v_r), (c, g), at(yhi=1 - yhi))

    def z3(c, g):
        _, direct, second = zsteps(c, g)
        for cp in direct + second:
            cp.wait_recv()
        r, w, h = rows[c], gcols[g], 1 - yhi
        for j in range(2):
            sy[j, r, w] = (own[h, j, r, w] + rz2[h, j, r, w].astype(F32) + rzd[h, j, r, w].astype(F32)).astype(BF16)
        go(vcopy(c, g))

    def out(c, g):
        vcopy(c, g).wait_recv()
        r, (a, b) = rows[c], span[g]
        for j in range(2):
            def total(o):
                w = pl.ds(2 * a + o * (b - a), b - a)
                return (own[yhi, j, r, w] + rz2[yhi, j, r, w].astype(F32)
                        + rzd[yhi, j, r, w].astype(F32) + ryz[j, r, w].astype(F32))
            v, u = total(0), total(1)
            hid[j, r, pl.ds(a, b - a)] = v / (1.0 + jnp.exp(-v)) * u
        cp = pltpu.make_async_copy(hid.at[:, r, pl.ds(a, b - a)], hid_h.at[:, r, pl.ds(a, b - a)], st.at[1 + g, c])
        cp.start()
        outs.append(cp)

    outs = []
    def grouped(f):
        return [functools.partial(f, g=0), functools.partial(f, g=1)]
    stage = [s_heads, s_proj, s_pair, s_x2, s_x3, s_res, s_norm, s_g2, s_g3, s_gath,
             *grouped(mlp), *grouped(z2), *grouped(z3), *grouped(out)]
    for s, c in ORDER:
        stage[s](c)
    for cp in sends:
        cp.make().wait_send()
    for cp in outs:
        cp.wait()


def handover(res_h, hid_h, res_o, hid_o, res_v, hid_v, sem):
    def moves(way, src, dst, k):
        n = src.shape[0] // HAND
        return [pltpu.make_async_copy(src.at[pl.ds(i * n, n)], dst.at[pl.ds(i * n, n)], sem.at[way, k, i])
                for i in range(HAND)]
    into = moves(0, res_h, res_v, 0) + moves(0, hid_h, hid_v, 1)
    back = moves(1, res_v, res_o, 0) + moves(1, hid_v, hid_o, 1)
    for cp in into:
        cp.start()
    for cp, nx in zip(into, back):
        cp.wait()
        nx.start()
    for cp in back:
        cp.wait()


def on_device(heads_output, residual_in, out_weight, norm_gain, gate_weight, up_weight):
    C = len(SIZES)
    dm, ffd = gate_weight.shape
    rows = residual_in.shape[0]
    anys = pl.BlockSpec(memory_space=pl.ANY)
    vm = pl.BlockSpec(memory_space=pltpu.VMEM)
    dma = pltpu.SemaphoreType.DMA
    V = pltpu.VMEM
    zb, zh = (2, 2, rows, 2 * ffd), (2, rows, 2 * ffd)
    res, hid = pl.pallas_call(
        functools.partial(body, C),
        out_shape=(jax.ShapeDtypeStruct((rows, dm), F32), jax.ShapeDtypeStruct((2, rows, ffd), F32)),
        in_specs=[anys, anys, anys, vm, anys, anys],
        out_specs=(anys, anys),
        scratch_shapes=[
            V((8, 2, rows, 512), BF16), V((512, dm), BF16), V((dm, 2 * ffd), BF16), V((rows, dm), BF16),
            V((8, rows, dm), F32), V((8, rows, dm), F32), V((8, rows, dm), F32),
            V((2, rows, dm), F32), V((2, rows, dm), F32), V((2, rows, dm), F32), V((rows, dm), F32),
            V((rows, dm), F32), V((8, rows, 128), F32), V((8, 2, rows, dm), BF16),
            V(zb, BF16), V(zh, BF16), V(zh, BF16), V(zh, F32), V(zh, F32), V(zb, F32), V(zb, BF16), V(zb, BF16), V(zb, BF16),
            V((2, rows, 2 * ffd), BF16), V((2, rows, 2 * ffd), BF16), V((2, rows, ffd), F32),
            dma((7,)), dma((3, C)), dma((C, 7)), dma((C, 7)), dma((C,)), dma((C,)), dma((C, 6)), dma((C, 6)),
            dma((C,)), dma((C,)), dma((C, 7)), dma((C, 7)), dma((C, 7)), dma((C, 7)), dma((C, 8)), dma((C, 8)),
            dma((C, 2, 6)), dma((C, 2, 6)), dma((C, 2)), dma((C, 2)),
        ],
        compiler_params=pltpu.CompilerParams(collective_id=0, has_side_effects=True, vmem_limit_bytes=62 << 20),
        name="layer",
    )(heads_output.reshape(2, rows, 512), residual_in, out_weight, norm_gain.reshape(1, dm), gate_weight, up_weight)
    out = (jax.ShapeDtypeStruct(res.shape, F32), jax.ShapeDtypeStruct((2 * rows, ffd), F32))
    return pl.pallas_call(
        handover, out_shape=out, in_specs=[anys, anys], out_specs=(anys, anys),
        scratch_shapes=[V(res.shape, F32), V((2 * rows, ffd), F32), dma((2, 2, HAND))], name="handover",
    )(res, hid.reshape(2 * rows, ffd))


def solution(mesh):
    return jax.shard_map(
        on_device, mesh=mesh,
        in_specs=(P("narrow", "wide"), P("wide", "narrow"), P("wide", "narrow"), P("narrow"),
                  P("narrow", "wide"), P("narrow", "wide")),
        out_specs=(P("wide", "narrow"), P("narrow", "wide")), check_vma=False)
```
